32 devices in a mesh: groups: 2 (over x), seq: 16 (over z, y, core).
Axes of the slice: x: 2, y: 2, z: 4, core: 2. Of those that a mesh axis runs over, the one named last changes fastest.
Arguments:
- queries: bfloat16 [64, 4, 8192], P(('groups', 'seq')), parts along dimension 0, may hold values from -128 to 128
- step_keys: bfloat16 [64, 4, 1024], P(('groups', 'seq')), parts along dimension 0, may hold values from -15 to 15
- step_values: bfloat16 [64, 4, 1024], P(('groups', 'seq')), parts along dimension 0, may hold values from -48 to 48
- sample_keys: bfloat16 [64, 1024, 1024], P(('groups', 'seq')), parts along dimension 0, may hold values from -6 to 6
- sample_values: bfloat16 [64, 1024, 1024], P(('groups', 'seq')), parts along dimension 0, may hold values from -48 to 48
- suffix_len: int32 [64], P(('groups', 'seq')), parts along dimension 0, may hold values from 128 to 1024
- prompt_id: int32 [64], P(('groups', 'seq')), parts along dimension 0, may hold values from 0 to 1, as said below
- document_keys: bfloat16 [4, 4096, 1024], P('groups', 'seq'), parts along dimension 0, may hold values from -6 to 6
- document_values: bfloat16 [4, 4096, 1024], P('groups', 'seq'), parts along dimension 0, may hold values from -48 to 48
Outputs:
- attended: bfloat16 [64, 4, 8192], P(('groups', 'seq')), parts along dimension 0
The draws below stay inside these ranges and needn't reach their ends.
There are 2 independent parts, one for each index of `groups`. The reference program is written for one: setup_inputs(seed, part) draws one part's arguments, and reference() takes and returns one part's arrays. A program takes and returns all parts, laid end to end along the dimension named above; each array names one. Nothing has to cross between parts.
Inputs may be any that keep to these rules, and one draw needn't show every extreme that they name: `prompt_id`: each prompt id is held by exactly 16 samples.
All inputs are finite; a program needn't handle non-finite values.
Results may differ from the reference program's by a relative error of at most 0.0013.
Values may be sent and summed in bfloat16 or wider, within the bound.
A program may use at most 192 MiB of HBM per device.

```python
import jax
import jax.numpy as jnp
from jax import lax

QUERY_HEADS = 64
KEY_VALUE_HEADS = 8
HEAD_SIZE = 128
GROUP_PROMPTS = 2
DECODE_STEPS = 4
BLOCK_PREFIX = 256
SUFFIX_SLOTS = 1024
GROUP_SAMPLES = 32
PREFIX_LENGTH = 4096


def draw_queries(key, part):
    leading_key = jax.random.fold_in(jax.random.fold_in(key, 101), 0)
    entry_list = jnp.clip(2.0 * jax.random.normal(leading_key, (GROUP_SAMPLES, DECODE_STEPS, QUERY_HEADS, HEAD_SIZE), jnp.float32), -12.0, 12.0)
    return entry_list.reshape(GROUP_SAMPLES, DECODE_STEPS, QUERY_HEADS * HEAD_SIZE).astype(jnp.bfloat16)


def draw_document_keys(key, part):
    leading_key = jax.random.fold_in(key, 202)
    entry_list = jnp.clip(jax.random.normal(leading_key, (GROUP_PROMPTS, PREFIX_LENGTH, KEY_VALUE_HEADS, HEAD_SIZE), jnp.float32), -6.0, 6.0)
    return entry_list.reshape(GROUP_PROMPTS, PREFIX_LENGTH, KEY_VALUE_HEADS * HEAD_SIZE).astype(jnp.bfloat16)


def draw_prompt_id(key, part):
    shuffled = jax.random.permutation(jax.random.fold_in(key, 303), GROUP_SAMPLES)
    return (shuffled // (GROUP_SAMPLES // GROUP_PROMPTS)).astype(jnp.int32)


def with_ends(entries, key, low, high):
    spot = [jax.random.randint(jax.random.fold_in(key, axis), (), 0, length) for axis, length in enumerate(entries.shape)]
    widest = entries.shape.index(max(entries.shape))
    beside = spot[:widest] + [(spot[widest] + 1) % entries.shape[widest]] + spot[widest + 1:]
    return entries.at[tuple(spot)].set(low).at[tuple(beside)].set(high)


def block_scale(stream_key, dims, cuts, least, top_value):
    loudness = 1.0
    for dim, parts in cuts:
        draws = jax.random.uniform(jax.random.fold_in(jax.random.fold_in(stream_key, 6), dim), (parts,), jnp.float32, least / len(cuts), top_value / len(cuts))
        loudness = loudness * jnp.repeat(jnp.exp(draws), dims[dim] // parts).reshape((-1,) + (1,) * (len(dims) - 1 - dim))
    return loudness


def centred(own_key, extent, scale, most, cuts=(), held_as=jnp.bfloat16):
    result = jax.random.normal(own_key, extent, jnp.float32) * scale
    if len(cuts) > 0:
        result = block_scale(own_key, extent, cuts, -0.22, 0.18) * result
    return jnp.clip(result, min=-most, max=most).astype(held_as)


def setup_inputs(seed: int = 0, part: int = 0) -> dict:
    keys = jax.random.split(jax.random.key(seed), 10)
    part_splits = jax.random.split(jax.random.fold_in(keys[9], part), 10)
    queries = draw_queries(jax.random.fold_in(jax.random.fold_in(keys[9], part), 71), part)
    step_keys = centred(part_splits[1], (GROUP_SAMPLES, DECODE_STEPS, KEY_VALUE_HEADS * HEAD_SIZE), 2.5, 15.0, ((0, 16),))
    step_values = centred(part_splits[2], (GROUP_SAMPLES, DECODE_STEPS, KEY_VALUE_HEADS * HEAD_SIZE), 8.0, 48.0, ((0, 16),))
    sample_keys = centred(part_splits[3], (GROUP_SAMPLES, SUFFIX_SLOTS, KEY_VALUE_HEADS * HEAD_SIZE), 1.0, 6.0, ((0, 16),))
    sample_values = centred(part_splits[4], (GROUP_SAMPLES, SUFFIX_SLOTS, KEY_VALUE_HEADS * HEAD_SIZE), 8.0, 48.0, ((0, 16),))
    suffix_len = with_ends(jax.random.randint(part_splits[5], (GROUP_SAMPLES,), SUFFIX_SLOTS // 8, SUFFIX_SLOTS + 1), jax.random.fold_in(part_splits[5], 1), SUFFIX_SLOTS // 8, SUFFIX_SLOTS).astype(jnp.int32)
    prompt_id = draw_prompt_id(jax.random.fold_in(jax.random.fold_in(keys[9], part), 71), part)
    document_keys = draw_document_keys(jax.random.fold_in(jax.random.fold_in(keys[9], part), 71), part)
    document_values = centred(part_splits[8], (GROUP_PROMPTS, PREFIX_LENGTH, KEY_VALUE_HEADS * HEAD_SIZE), 8.0, 48.0, ((1, 16),))
    return dict(queries=queries, step_keys=step_keys, step_values=step_values, sample_keys=sample_keys, sample_values=sample_values, suffix_len=suffix_len, prompt_id=prompt_id, document_keys=document_keys, document_values=document_values)


def rounded(values):
    return lax.optimization_barrier(values.astype(jnp.bfloat16)).astype(jnp.float32)


def reference(queries, step_keys, step_values, sample_keys, sample_values, suffix_len, prompt_id, document_keys, document_values):
    group_count = QUERY_HEADS // KEY_VALUE_HEADS
    block_list = PREFIX_LENGTH // BLOCK_PREFIX
    scaling = HEAD_SIZE ** -0.5

    def per_sample(members):
        query_vector, recent_key_rows, recent_value_rows, cache_key_rows, cache_value_rows, length, prompt_row = members
        query_matrix = query_vector.astype(jnp.float32).reshape(DECODE_STEPS, KEY_VALUE_HEADS, group_count, HEAD_SIZE)
        present_keys = lax.dynamic_index_in_dim(document_keys, prompt_row, 0, keepdims=False)
        present_values = lax.dynamic_index_in_dim(document_values, prompt_row, 0, keepdims=False)
        present_keys = present_keys.astype(jnp.float32).reshape(block_list, BLOCK_PREFIX, KEY_VALUE_HEADS, HEAD_SIZE)
        present_values = present_values.astype(jnp.float32).reshape(block_list, BLOCK_PREFIX, KEY_VALUE_HEADS, HEAD_SIZE)
        prefix_score = jnp.einsum('tgrd,bkgd->btgrk', query_matrix, present_keys) * scaling
        prefix_max = jnp.max(prefix_score, axis=-1)
        prefix_exp = jnp.exp(prefix_score - prefix_max[..., None])
        prefix_total = jnp.sum(prefix_exp, axis=-1)
        prefix_out = jnp.einsum('btgrk,bkgd->btgrd', rounded(prefix_exp), present_values)

        cached_key_set = cache_key_rows.astype(jnp.float32).reshape(SUFFIX_SLOTS, KEY_VALUE_HEADS, HEAD_SIZE)
        cached_value_set = cache_value_rows.astype(jnp.float32).reshape(SUFFIX_SLOTS, KEY_VALUE_HEADS, HEAD_SIZE)
        recent_keys = recent_key_rows.astype(jnp.float32).reshape(DECODE_STEPS, KEY_VALUE_HEADS, HEAD_SIZE)
        recent_values = recent_value_rows.astype(jnp.float32).reshape(DECODE_STEPS, KEY_VALUE_HEADS, HEAD_SIZE)
        cache_score = jnp.einsum('tgrd,kgd->tgrk', query_matrix, cached_key_set) * scaling
        fresh_score = jnp.einsum('tgrd,ugd->tgru', query_matrix, recent_keys) * scaling
        cache_live = (jnp.arange(SUFFIX_SLOTS, dtype=jnp.int32) < length)[None, None, None, :]
        fresh_live = (jnp.arange(DECODE_STEPS)[None, :] <= jnp.arange(DECODE_STEPS)[:, None])[:, None, None, :]
        suffix_max = jnp.maximum(jnp.max(jnp.where(cache_live, cache_score, -jnp.inf), axis=-1),
                                 jnp.max(jnp.where(fresh_live, fresh_score, -jnp.inf), axis=-1))
        cache_exp = jnp.where(cache_live, jnp.exp(cache_score - suffix_max[..., None]), 0.0)
        fresh_exp = jnp.where(fresh_live, jnp.exp(fresh_score - suffix_max[..., None]), 0.0)
        suffix_total = jnp.sum(cache_exp, axis=-1) + jnp.sum(fresh_exp, axis=-1)
        suffix_out = (jnp.einsum('tgrk,kgd->tgrd', rounded(cache_exp), cached_value_set)
                      + jnp.einsum('tgru,ugd->tgrd', rounded(fresh_exp), recent_values))

        highest = jnp.maximum(jnp.max(prefix_max, axis=0), suffix_max)
        prefix_scale = jnp.exp(prefix_max - highest[None])
        suffix_scale = jnp.exp(suffix_max - highest)
        numerator = jnp.sum(prefix_out * prefix_scale[..., None], axis=0) + suffix_out * suffix_scale[..., None]
        denominator = jnp.sum(prefix_total * prefix_scale, axis=0) + suffix_total * suffix_scale
        return (numerator / denominator[..., None]).reshape(DECODE_STEPS, QUERY_HEADS * HEAD_SIZE).astype(jnp.bfloat16)

    return lax.map(per_sample, (queries, step_keys, step_values, sample_keys, sample_values, suffix_len, prompt_id))
```

```python
import functools

import jax
import jax.numpy as jnp
from jax import lax
from jax.experimental import pallas as pl
from jax.experimental.pallas import tpu as pltpu
from jax.sharding import PartitionSpec as P

QUERY_HEADS = 64
KEY_VALUE_HEADS = 8
HEAD_SIZE = 128
LOG2E = 1.4426950408889634
ID_ROWS = 16
STAT_ROWS = 8
MESH = pl.DeviceIdType.MESH
NT = (((1,), (1,)), ((), ()))
NN = (((1,), (0,)), ((), ()))


def member(head, offset):
    result = 0
    for bit in range(3):
        weight = 1 << bit
        own = lax.rem(head // weight, 2)
        result = result + weight * (1 - own if offset & weight else own)
    return result


def kernel(
    n,
    len_ref,
    query_ref,
    step_key_ref,
    step_value_ref,
    sample_keys,
    sample_values,
    document_keys,
    document_values,
    out_ref,
    key_buf,
    value_buf,
    head_keys,
    head_values,
    query_buf,
    query_cat,
    id_buf,
    acc,
    acc_max,
    acc_total,
    send_buf,
    got_buf,
    own_out,
    own_max,
    own_total,
    local_sem,
    query_send,
    query_recv,
    pair_send,
    pair_recv,
    part_send,
    part_recv,
):
    me = lax.axis_index("seq")
    my_head = lax.rem(me, KEY_VALUE_HEADS)
    my_base = me - my_head
    samples, cache = sample_keys.shape[0], sample_keys.shape[1]
    steps = step_key_ref.shape[1]
    rows = query_ref.shape[2] - ID_ROWS
    owner_rows = samples * rows
    prompts = document_keys.shape[0]
    padded = key_buf.shape[1]
    factor = (HEAD_SIZE ** (-0.5)) * LOG2E

    def columns(head):
        return pl.ds(pl.multiple_of(head * HEAD_SIZE, HEAD_SIZE), HEAD_SIZE)

    local = [
        pltpu.make_async_copy(
            sample_keys, key_buf.at[:, pl.ds(0, cache), :], local_sem.at[0]
        ),
        pltpu.make_async_copy(
            sample_values, value_buf.at[:, pl.ds(0, cache), :], local_sem.at[1]
        ),
        pltpu.make_async_copy(
            document_keys.at[:, :, columns(my_head)], head_keys.at[0], local_sem.at[2]
        ),
        pltpu.make_async_copy(
            document_values.at[:, :, columns(my_head)], head_values.at[0], local_sem.at[3]
        ),
    ]
    for copy in local:
        copy.start()

    barrier = pltpu.get_barrier_semaphore()

    def greet(step, carry):
        other = lax.rem(me + step, n)
        pl.semaphore_signal(barrier, inc=1, device_id={"seq": other}, device_id_type=MESH)
        return carry

    lax.fori_loop(1, n, greet, 0)
    pl.semaphore_wait(barrier, n - 1)

    def send_query(step, carry):
        other = lax.rem(me + step, n)
        pltpu.make_async_remote_copy(
            src_ref=query_ref.at[lax.rem(other, KEY_VALUE_HEADS)],
            dst_ref=query_buf.at[me],
            send_sem=query_send,
            recv_sem=query_recv,
            device_id={"seq": other},
            device_id_type=MESH,
        ).start()
        return carry

    lax.fori_loop(1, n, send_query, 0)

    pairs = {}
    for offset in (6, 7, 4, 5, 2, 3, 1):
        head = member(my_head, offset)
        for kind, (source, target) in enumerate(
            ((document_keys, head_keys), (document_values, head_values))
        ):
            copy = pltpu.make_async_remote_copy(
                src_ref=source.at[:, :, columns(head)],
                dst_ref=target.at[offset],
                send_sem=pair_send.at[kind, offset],
                recv_sem=pair_recv.at[kind, offset],
                device_id={"seq": my_base + head},
                device_id_type=MESH,
            )
            copy.start()
            pairs[kind, offset] = copy

    query_buf[me] = query_ref[my_head]
    for s in range(samples):
        key_buf[s, pl.ds(cache, padded - cache), :] = jnp.zeros(
            (padded - cache, key_buf.shape[2]), key_buf.dtype
        )
        value_buf[s, pl.ds(cache, padded - cache), :] = jnp.zeros(
            (padded - cache, value_buf.shape[2]), value_buf.dtype
        )
        key_buf[s, pl.ds(cache, steps), :] = step_key_ref[s]
        value_buf[s, pl.ds(cache, steps), :] = step_value_ref[s]
    for copy in local:
        copy.wait()

    slot = lax.broadcasted_iota(jnp.int32, (rows, padded), 1)
    now = lax.broadcasted_iota(jnp.int32, (rows, padded), 0) // (rows // steps)
    fresh = (slot >= cache) & (slot - cache <= now)

    def suffix_head(head, carry):
        for s in range(samples):
            query = query_ref[head, s, pl.ds(0, rows), :]
            scores = lax.dot_general(
                query, key_buf[s, :, columns(head)], NT, preferred_element_type=jnp.float32
            )
            live = (slot < len_ref[s]) | fresh
            scores = jnp.where(live, scores, -jnp.inf)
            peak = jnp.max(scores, axis=1, keepdims=True)
            expo = jnp.exp2((scores - peak) * factor)
            part = pl.ds(s * rows, rows)
            own_max[head, part, :] = peak
            own_total[head, part, :] = jnp.sum(expo, axis=1, keepdims=True)
            own_out[head, part, :] = lax.dot_general(
                expo.astype(jnp.bfloat16),
                value_buf[s, :, columns(head)],
                NN,
                preferred_element_type=jnp.float32,
            )
        return carry

    lax.fori_loop(0, KEY_VALUE_HEADS, suffix_head, 0)

    others = query_buf.at[pl.ds(0, n - 1)]
    pltpu.make_async_copy(others, others, query_recv).wait()

    def place(source, carry):
        for s in range(samples):
            query = query_buf[source, s, pl.ds(0, rows), :].astype(jnp.float32)
            mark = query_buf[source, s, pl.ds(rows, ID_ROWS), :].astype(jnp.float32)
            mark = jnp.concatenate([mark] * (rows // ID_ROWS), axis=0)
            part = pl.ds(pl.multiple_of(source * owner_rows + s * rows, rows), rows)
            for p in range(prompts):
                query_cat[part, pl.ds(p * HEAD_SIZE, HEAD_SIZE)] = jnp.where(
                    mark == p, query, 0.0
                ).astype(jnp.bfloat16)
            id_buf[part, :] = mark
            acc[part, :] = jnp.zeros((rows, HEAD_SIZE), jnp.float32)
            acc_max[part, :] = jnp.full((rows, 1), -1e30, jnp.float32)
            acc_total[part, :] = jnp.zeros((rows, 1), jnp.float32)
        return carry

    lax.fori_loop(0, n, place, 0)

    owners = 4 if n % 4 == 0 else 1
    chunk = owners * owner_rows

    def attend(offset, index):
        part = pl.ds(pl.multiple_of(index * chunk, chunk), chunk)
        keys = jnp.concatenate([head_keys[offset, p] for p in range(prompts)], axis=1)
        values = jnp.concatenate([head_values[offset, p] for p in range(prompts)], axis=1)
        scores = lax.dot_general(
            query_cat[part, :], keys, NT, preferred_element_type=jnp.float32
        )
        peak = jnp.max(scores, axis=1, keepdims=True)
        expo = jnp.exp2((scores - peak) * factor)
        total = jnp.sum(expo, axis=1, keepdims=True)
        both = lax.dot_general(
            expo.astype(jnp.bfloat16), values, NN, preferred_element_type=jnp.float32
        )
        mark = id_buf[part, :]
        result = both[:, :HEAD_SIZE]
        for p in range(1, prompts):
            result = jnp.where(
                mark == p, both[:, p * HEAD_SIZE : (p + 1) * HEAD_SIZE], result
            )
        before = acc_max[part, :]
        top = jnp.maximum(before, peak)
        old = jnp.exp2((before - top) * factor)
        new = jnp.exp2((peak - top) * factor)
        return part, acc[part, :] * old + result * new, top, acc_total[part, :] * old + total * new

    def keep(offset, index):
        part, merged, top, total = attend(offset, index)
        acc[part, :] = merged
        acc_max[part, :] = top
        acc_total[part, :] = total

    def over_block(offset, carry):
        lax.fori_loop(0, n // owners, lambda i, c: (keep(offset, i), c)[1], 0)
        return carry

    over_block(0, 0)
    last = KEY_VALUE_HEADS - 1
    for offset in range(1, last):
        pairs[0, offset].wait_recv()
        pairs[1, offset].wait_recv()
        over_block(offset, 0)
    pairs[0, last].wait_recv()
    pairs[1, last].wait_recv()

    diagonal = lax.broadcasted_iota(jnp.int32, (owner_rows, HEAD_SIZE), 0) == (
        lax.broadcasted_iota(jnp.int32, (owner_rows, HEAD_SIZE), 1)
    )
    stat_row = lax.broadcasted_iota(jnp.int32, (STAT_ROWS, HEAD_SIZE), 0)

    def finish(index, carry):
        _, merged, top, total = attend(last, index)
        for j in range(owners):
            owner = index * owners + j
            cut = slice(j * owner_rows, (j + 1) * owner_rows)
            send_buf[owner, pl.ds(0, owner_rows), :] = merged[cut]
            peak_row = jnp.sum(jnp.where(diagonal, top[cut], 0.0), axis=0, keepdims=True)
            total_row = jnp.sum(jnp.where(diagonal, total[cut], 0.0), axis=0, keepdims=True)
            send_buf[owner, pl.ds(owner_rows, STAT_ROWS), :] = jnp.where(
                stat_row == 0, peak_row, jnp.where(stat_row == 1, total_row, 0.0)
            )

            @pl.when(owner != me)
            def _():
                pltpu.make_async_remote_copy(
                    src_ref=send_buf.at[owner],
                    dst_ref=got_buf.at[me],
                    send_sem=part_send,
                    recv_sem=part_recv,
                    device_id={"seq": owner},
                    device_id_type=MESH,
                ).start()

        return carry

    lax.fori_loop(0, n // owners, finish, 0)
    got_buf[me] = send_buf[me]
    others = got_buf.at[pl.ds(0, n - 1)]
    pltpu.make_async_copy(others, others, part_recv).wait()

    def merge(head, carry):
        top = own_max[head]
        parts = []
        for group in range(n // KEY_VALUE_HEADS):
            source = group * KEY_VALUE_HEADS + head
            stats = got_buf[source, pl.ds(owner_rows, STAT_ROWS), :]
            peak = jnp.sum(jnp.where(diagonal, stats[0:1], 0.0), axis=1, keepdims=True)
            total = jnp.sum(jnp.where(diagonal, stats[1:2], 0.0), axis=1, keepdims=True)
            parts.append((source, peak, total))
            top = jnp.maximum(top, peak)
        weight = jnp.exp2((own_max[head] - top) * factor)
        above = own_out[head] * weight
        below = own_total[head] * weight
        for source, peak, total in parts:
            weight = jnp.exp2((peak - top) * factor)
            above = above + got_buf[source, pl.ds(0, owner_rows), :] * weight
            below = below + total * weight
        out_ref[head] = (above / below).astype(out_ref.dtype)
        return carry

    lax.fori_loop(0, KEY_VALUE_HEADS, merge, 0)

    sent = query_buf.at[pl.ds(0, n - 1)]
    pltpu.make_async_copy(sent, sent, query_send).wait()
    sent = send_buf.at[pl.ds(0, n - 1)]
    pltpu.make_async_copy(sent, sent, part_send).wait()
    for copy in pairs.values():
        copy.wait_send()


def body(
    queries,
    step_keys,
    step_values,
    sample_keys,
    sample_values,
    suffix_len,
    prompt_id,
    document_keys,
    document_values,
):
    n = lax.axis_size("seq")
    samples, steps = queries.shape[:2]
    cache = sample_keys.shape[1]
    width = KEY_VALUE_HEADS * HEAD_SIZE
    prompts, block = document_keys.shape[:2]
    group = QUERY_HEADS // KEY_VALUE_HEADS
    rows = steps * group
    owner_rows = samples * rows
    total_rows = n * owner_rows
    padded = cache + 128
    by_head = queries.reshape(samples, steps, KEY_VALUE_HEADS, group, HEAD_SIZE)
    by_head = by_head.transpose(2, 0, 1, 3, 4).reshape(KEY_VALUE_HEADS, samples, rows, HEAD_SIZE)
    marks = jnp.broadcast_to(
        prompt_id.astype(jnp.bfloat16)[None, :, None, None],
        (KEY_VALUE_HEADS, samples, ID_ROWS, HEAD_SIZE),
    )
    messages = jnp.concatenate([by_head, marks], axis=2)
    f32, bf16 = jnp.float32, jnp.bfloat16
    vmem = pl.BlockSpec(memory_space=pltpu.VMEM)
    hbm = pl.BlockSpec(memory_space=pl.ANY)
    dma = pltpu.SemaphoreType.DMA
    result = pl.pallas_call(
        functools.partial(kernel, n),
        out_shape=jax.ShapeDtypeStruct((KEY_VALUE_HEADS, owner_rows, HEAD_SIZE), bf16),
        in_specs=[pl.BlockSpec(memory_space=pltpu.SMEM), vmem, vmem, vmem, hbm, hbm, hbm, hbm],
        out_specs=vmem,
        scratch_shapes=[
            pltpu.VMEM((samples, padded, width), bf16),
            pltpu.VMEM((samples, padded, width), bf16),
            pltpu.VMEM((KEY_VALUE_HEADS, prompts, block, HEAD_SIZE), bf16),
            pltpu.VMEM((KEY_VALUE_HEADS, prompts, block, HEAD_SIZE), bf16),
            pltpu.VMEM((n, samples, rows + ID_ROWS, HEAD_SIZE), bf16),
            pltpu.VMEM((total_rows, prompts * HEAD_SIZE), bf16),
            pltpu.VMEM((total_rows, HEAD_SIZE), f32),
            pltpu.VMEM((total_rows, HEAD_SIZE), f32),
            pltpu.VMEM((total_rows, 1), f32),
            pltpu.VMEM((total_rows, 1), f32),
            pltpu.VMEM((n, owner_rows + STAT_ROWS, HEAD_SIZE), f32),
            pltpu.VMEM((n, owner_rows + STAT_ROWS, HEAD_SIZE), f32),
            pltpu.VMEM((KEY_VALUE_HEADS, owner_rows, HEAD_SIZE), f32),
            pltpu.VMEM((KEY_VALUE_HEADS, owner_rows, 1), f32),
            pltpu.VMEM((KEY_VALUE_HEADS, owner_rows, 1), f32),
            dma((4,)),
            dma,
            dma,
            dma((2, KEY_VALUE_HEADS)),
            dma((2, KEY_VALUE_HEADS)),
            dma,
            dma,
        ],
        compiler_params=pltpu.CompilerParams(
            collective_id=0, has_side_effects=True, vmem_limit_bytes=60 << 20
        ),
    )(
        suffix_len,
        messages,
        step_keys,
        step_values,
        sample_keys,
        sample_values,
        document_keys,
        document_values,
    )
    result = result.reshape(KEY_VALUE_HEADS, samples, steps, group, HEAD_SIZE)
    return result.transpose(1, 2, 0, 3, 4).reshape(samples, steps, QUERY_HEADS * HEAD_SIZE)


def solution(mesh):
    return jax.shard_map(
        body,
        mesh=mesh,
        in_specs=(
            P(("groups", "seq"), None, None),
            P(("groups", "seq"), None, None),
            P(("groups", "seq"), None, None),
            P(("groups", "seq"), None, None),
            P(("groups", "seq"), None, None),
            P(("groups", "seq")),
            P(("groups", "seq")),
            P("groups", "seq", None),
            P("groups", "seq", None),
        ),
        out_specs=P(("groups", "seq"), None, None),
        check_vma=False,
    )
```

```python
import functools

import jax
import jax.numpy as jnp
from jax import lax
from jax.experimental import pallas as pl
from jax.experimental.pallas import tpu as pltpu
from jax.sharding import PartitionSpec as P

QUERY_HEADS = 64
KEY_VALUE_HEADS = 8
HEAD_SIZE = 128
LOG2E = 1.4426950408889634
ID_ROWS = 16
STAT_ROWS = 8
MESH = pl.DeviceIdType.MESH
NT = (((1,), (1,)), ((), ()))
NN = (((1,), (0,)), ((), ()))


def member(head, offset):
    result = 0
    for bit in range(3):
        weight = 1 << bit
        own = lax.rem(head // weight, 2)
        result = result + weight * (1 - own if offset & weight else own)
    return result


def kernel(
    n,
    len_ref,
    query_ref,
    step_key_ref,
    step_value_ref,
    sample_keys,
    sample_values,
    document_keys,
    document_values,
    out_ref,
    key_buf,
    value_buf,
    head_keys,
    head_values,
    query_buf,
    query_cat,
    id_buf,
    acc,
    acc_max,
    acc_total,
    send_buf,
    got_buf,
    own_out,
    own_max,
    own_total,
    local_sem,
    query_send,
    query_recv,
    pair_send,
    pair_recv,
    part_send,
    part_recv,
):
    me = lax.axis_index("seq")
    my_head = lax.rem(me, KEY_VALUE_HEADS)
    my_base = me - my_head
    samples, cache = sample_keys.shape[0], sample_keys.shape[1]
    steps = step_key_ref.shape[1]
    rows = query_ref.shape[2] - ID_ROWS
    owner_rows = samples * rows
    prompts = document_keys.shape[0]
    padded = key_buf.shape[1]
    factor = (HEAD_SIZE ** (-0.5)) * LOG2E

    def columns(head):
        return pl.ds(pl.multiple_of(head * HEAD_SIZE, HEAD_SIZE), HEAD_SIZE)

    local = [
        pltpu.make_async_copy(
            sample_keys, key_buf.at[:, pl.ds(0, cache), :], local_sem.at[0]
        ),
        pltpu.make_async_copy(
            sample_values, value_buf.at[:, pl.ds(0, cache), :], local_sem.at[1]
        ),
        pltpu.make_async_copy(
            document_keys.at[:, :, columns(my_head)], head_keys.at[0], local_sem.at[2]
        ),
        pltpu.make_async_copy(
            document_values.at[:, :, columns(my_head)], head_values.at[0], local_sem.at[3]
        ),
    ]
    for copy in local:
        copy.start()

    barrier = pltpu.get_barrier_semaphore()

    def greet(step, carry):
        other = lax.rem(me + step, n)
        pl.semaphore_signal(barrier, inc=1, device_id={"seq": other}, device_id_type=MESH)
        return carry

    lax.fori_loop(1, n, greet, 0)
    pl.semaphore_wait(barrier, n - 1)

    def send_query(step, carry):
        other = lax.rem(me + step, n)
        pltpu.make_async_remote_copy(
            src_ref=query_ref.at[lax.rem(other, KEY_VALUE_HEADS)],
            dst_ref=query_buf.at[me],
            send_sem=query_send,
            recv_sem=query_recv,
            device_id={"seq": other},
            device_id_type=MESH,
        ).start()
        return carry

    lax.fori_loop(1, n, send_query, 0)

    pairs = {}
    for offset in (2, 4, 3, 5, 6, 7, 1):
        head = member(my_head, offset)
        for kind, (source, target) in enumerate(
            ((document_keys, head_keys), (document_values, head_values))
        ):
            copy = pltpu.make_async_remote_copy(
                src_ref=source.at[:, :, columns(head)],
                dst_ref=target.at[offset],
                send_sem=pair_send.at[kind, offset],
                recv_sem=pair_recv.at[kind, offset],
                device_id={"seq": my_base + head},
                device_id_type=MESH,
            )
            copy.start()
            pairs[kind, offset] = copy

    query_buf[me] = query_ref[my_head]
    for s in range(samples):
        key_buf[s, pl.ds(cache, padded - cache), :] = jnp.zeros(
            (padded - cache, key_buf.shape[2]), key_buf.dtype
        )
        value_buf[s, pl.ds(cache, padded - cache), :] = jnp.zeros(
            (padded - cache, value_buf.shape[2]), value_buf.dtype
        )
        key_buf[s, pl.ds(cache, steps), :] = step_key_ref[s]
        value_buf[s, pl.ds(cache, steps), :] = step_value_ref[s]
    for copy in local:
        copy.wait()

    slot = lax.broadcasted_iota(jnp.int32, (rows, padded), 1)
    now = lax.broadcasted_iota(jnp.int32, (rows, padded), 0) // (rows // steps)
    fresh = (slot >= cache) & (slot - cache <= now)

    def suffix_head(head, carry):
        for s in range(samples):
            query = query_ref[head, s, pl.ds(0, rows), :]
            scores = lax.dot_general(
                query, key_buf[s, :, columns(head)], NT, preferred_element_type=jnp.float32
            )
            live = (slot < len_ref[s]) | fresh
            scores = jnp.where(live, scores, -jnp.inf)
            peak = jnp.max(scores, axis=1, keepdims=True)
            expo = jnp.exp2((scores - peak) * factor)
            part = pl.ds(s * rows, rows)
            own_max[head, part, :] = peak
            own_total[head, part, :] = jnp.sum(expo, axis=1, keepdims=True)
            own_out[head, part, :] = lax.dot_general(
                expo.astype(jnp.bfloat16),
                value_buf[s, :, columns(head)],
                NN,
                preferred_element_type=jnp.float32,
            )
        return carry

    lax.fori_loop(0, KEY_VALUE_HEADS, suffix_head, 0)

    others = query_buf.at[pl.ds(0, n - 1)]
    pltpu.make_async_copy(others, others, query_recv).wait()

    def place(source, carry):
        for s in range(samples):
            query = query_buf[source, s, pl.ds(0, rows), :].astype(jnp.float32)
            mark = query_buf[source, s, pl.ds(rows, ID_ROWS), :].astype(jnp.float32)
            mark = jnp.concatenate([mark] * (rows // ID_ROWS), axis=0)
            part = pl.ds(pl.multiple_of(source * owner_rows + s * rows, rows), rows)
            for p in range(prompts):
                query_cat[part, pl.ds(p * HEAD_SIZE, HEAD_SIZE)] = jnp.where(
                    mark == p, query, 0.0
                ).astype(jnp.bfloat16)
            id_buf[part, :] = mark
            acc[part, :] = jnp.zeros((rows, HEAD_SIZE), jnp.float32)
            acc_max[part, :] = jnp.full((rows, 1), -1e30, jnp.float32)
            acc_total[part, :] = jnp.zeros((rows, 1), jnp.float32)
        return carry

    lax.fori_loop(0, n, place, 0)

    owners = 4 if n % 4 == 0 else 1
    chunk = owners * owner_rows

    def attend(offset, index):
        part = pl.ds(pl.multiple_of(index * chunk, chunk), chunk)
        keys = jnp.concatenate([head_keys[offset, p] for p in range(prompts)], axis=1)
        values = jnp.concatenate([head_values[offset, p] for p in range(prompts)], axis=1)
        scores = lax.dot_general(
            query_cat[part, :], keys, NT, preferred_element_type=jnp.float32
        )
        peak = jnp.max(scores, axis=1, keepdims=True)
        expo = jnp.exp2((scores - peak) * factor)
        total = jnp.sum(expo, axis=1, keepdims=True)
        both = lax.dot_general(
            expo.astype(jnp.bfloat16), values, NN, preferred_element_type=jnp.float32
        )
        mark = id_buf[part, :]
        result = both[:, :HEAD_SIZE]
        for p in range(1, prompts):
            result = jnp.where(
                mark == p, both[:, p * HEAD_SIZE : (p + 1) * HEAD_SIZE], result
            )
        before = acc_max[part, :]
        top = jnp.maximum(before, peak)
        old = jnp.exp2((before - top) * factor)
        new = jnp.exp2((peak - top) * factor)
        return part, acc[part, :] * old + result * new, top, acc_total[part, :] * old + total * new

    def keep(offset, index):
        part, merged, top, total = attend(offset, index)
        acc[part, :] = merged
        acc_max[part, :] = top
        acc_total[part, :] = total

    def over_block(offset, carry):
        lax.fori_loop(0, n // owners, lambda i, c: (keep(offset, i), c)[1], 0)
        return carry

    over_block(0, 0)
    last = KEY_VALUE_HEADS - 1
    for offset in range(1, last):
        pairs[0, offset].wait_recv()
        pairs[1, offset].wait_recv()
        over_block(offset, 0)
    pairs[0, last].wait_recv()
    pairs[1, last].wait_recv()

    diagonal = lax.broadcasted_iota(jnp.int32, (owner_rows, HEAD_SIZE), 0) == (
        lax.broadcasted_iota(jnp.int32, (owner_rows, HEAD_SIZE), 1)
    )
    stat_row = lax.broadcasted_iota(jnp.int32, (STAT_ROWS, HEAD_SIZE), 0)

    chunks = n // owners

    def finish(step, carry):
        index = lax.rem(me // owners + chunks // 2 + step, chunks)
        _, merged, top, total = attend(last, index)
        for j in range(owners):
            owner = index * owners + j
            cut = slice(j * owner_rows, (j + 1) * owner_rows)
            send_buf[owner, pl.ds(0, owner_rows), :] = merged[cut]
            peak_row = jnp.sum(jnp.where(diagonal, top[cut], 0.0), axis=0, keepdims=True)
            total_row = jnp.sum(jnp.where(diagonal, total[cut], 0.0), axis=0, keepdims=True)
            send_buf[owner, pl.ds(owner_rows, STAT_ROWS), :] = jnp.where(
                stat_row == 0, peak_row, jnp.where(stat_row == 1, total_row, 0.0)
            )

            @pl.when(owner != me)
            def _():
                pltpu.make_async_remote_copy(
                    src_ref=send_buf.at[owner],
                    dst_ref=got_buf.at[me],
                    send_sem=part_send,
                    recv_sem=part_recv,
                    device_id={"seq": owner},
                    device_id_type=MESH,
                ).start()

        return carry

    lax.fori_loop(0, n // owners, finish, 0)
    got_buf[me] = send_buf[me]
    others = got_buf.at[pl.ds(0, n - 1)]
    pltpu.make_async_copy(others, others, part_recv).wait()

    def merge(head, carry):
        top = own_max[head]
        parts = []
        for group in range(n // KEY_VALUE_HEADS):
            source = group * KEY_VALUE_HEADS + head
            stats = got_buf[source, pl.ds(owner_rows, STAT_ROWS), :]
            peak = jnp.sum(jnp.where(diagonal, stats[0:1], 0.0), axis=1, keepdims=True)
            total = jnp.sum(jnp.where(diagonal, stats[1:2], 0.0), axis=1, keepdims=True)
            parts.append((source, peak, total))
            top = jnp.maximum(top, peak)
        weight = jnp.exp2((own_max[head] - top) * factor)
        above = own_out[head] * weight
        below = own_total[head] * weight
        for source, peak, total in parts:
            weight = jnp.exp2((peak - top) * factor)
            above = above + got_buf[source, pl.ds(0, owner_rows), :] * weight
            below = below + total * weight
        out_ref[head] = (above / below).astype(out_ref.dtype)
        return carry

    lax.fori_loop(0, KEY_VALUE_HEADS, merge, 0)

    sent = query_buf.at[pl.ds(0, n - 1)]
    pltpu.make_async_copy(sent, sent, query_send).wait()
    sent = send_buf.at[pl.ds(0, n - 1)]
    pltpu.make_async_copy(sent, sent, part_send).wait()
    for copy in pairs.values():
        copy.wait_send()


def body(
    queries,
    step_keys,
    step_values,
    sample_keys,
    sample_values,
    suffix_len,
    prompt_id,
    document_keys,
    document_values,
):
    n = lax.axis_size("seq")
    samples, steps = queries.shape[:2]
    cache = sample_keys.shape[1]
    width = KEY_VALUE_HEADS * HEAD_SIZE
    prompts, block = document_keys.shape[:2]
    group = QUERY_HEADS // KEY_VALUE_HEADS
    rows = steps * group
    owner_rows = samples * rows
    total_rows = n * owner_rows
    padded = cache + 128
    by_head = queries.reshape(samples, steps, KEY_VALUE_HEADS, group, HEAD_SIZE)
    by_head = by_head.transpose(2, 0, 1, 3, 4).reshape(KEY_VALUE_HEADS, samples, rows, HEAD_SIZE)
    marks = jnp.broadcast_to(
        prompt_id.astype(jnp.bfloat16)[None, :, None, None],
        (KEY_VALUE_HEADS, samples, ID_ROWS, HEAD_SIZE),
    )
    messages = jnp.concatenate([by_head, marks], axis=2)
    f32, bf16 = jnp.float32, jnp.bfloat16
    vmem = pl.BlockSpec(memory_space=pltpu.VMEM)
    hbm = pl.BlockSpec(memory_space=pl.ANY)
    dma = pltpu.SemaphoreType.DMA
    result = pl.pallas_call(
        functools.partial(kernel, n),
        out_shape=jax.ShapeDtypeStruct((KEY_VALUE_HEADS, owner_rows, HEAD_SIZE), bf16),
        in_specs=[pl.BlockSpec(memory_space=pltpu.SMEM), vmem, vmem, vmem, hbm, hbm, hbm, hbm],
        out_specs=vmem,
        scratch_shapes=[
            pltpu.VMEM((samples, padded, width), bf16),
            pltpu.VMEM((samples, padded, width), bf16),
            pltpu.VMEM((KEY_VALUE_HEADS, prompts, block, HEAD_SIZE), bf16),
            pltpu.VMEM((KEY_VALUE_HEADS, prompts, block, HEAD_SIZE), bf16),
            pltpu.VMEM((n, samples, rows + ID_ROWS, HEAD_SIZE), bf16),
            pltpu.VMEM((total_rows, prompts * HEAD_SIZE), bf16),
            pltpu.VMEM((total_rows, HEAD_SIZE), f32),
            pltpu.VMEM((total_rows, HEAD_SIZE), f32),
            pltpu.VMEM((total_rows, 1), f32),
            pltpu.VMEM((total_rows, 1), f32),
            pltpu.VMEM((n, owner_rows + STAT_ROWS, HEAD_SIZE), f32),
            pltpu.VMEM((n, owner_rows + STAT_ROWS, HEAD_SIZE), f32),
            pltpu.VMEM((KEY_VALUE_HEADS, owner_rows, HEAD_SIZE), f32),
            pltpu.VMEM((KEY_VALUE_HEADS, owner_rows, 1), f32),
            pltpu.VMEM((KEY_VALUE_HEADS, owner_rows, 1), f32),
            dma((4,)),
            dma,
            dma,
            dma((2, KEY_VALUE_HEADS)),
            dma((2, KEY_VALUE_HEADS)),
            dma,
            dma,
        ],
        compiler_params=pltpu.CompilerParams(
            collective_id=0, has_side_effects=True, vmem_limit_bytes=60 << 20
        ),
    )(
        suffix_len,
        messages,
        step_keys,
        step_values,
        sample_keys,
        sample_values,
        document_keys,
        document_values,
    )
    result = result.reshape(KEY_VALUE_HEADS, samples, steps, group, HEAD_SIZE)
    return result.transpose(1, 2, 0, 3, 4).reshape(samples, steps, QUERY_HEADS * HEAD_SIZE)


def solution(mesh):
    return jax.shard_map(
        body,
        mesh=mesh,
        in_specs=(
            P(("groups", "seq"), None, None),
            P(("groups", "seq"), None, None),
            P(("groups", "seq"), None, None),
            P(("groups", "seq"), None, None),
            P(("groups", "seq"), None, None),
            P(("groups", "seq")),
            P(("groups", "seq")),
            P("groups", "seq", None),
            P("groups", "seq", None),
        ),
        out_specs=P(("groups", "seq"), None, None),
        check_vma=False,
    )
```
